32 devices in a mesh: row: 8 (over z, core), col: 4 (over y, x).
Axes of the slice: x: 2, y: 2, z: 4, core: 2. Of those that a mesh axis runs over, the one named last changes fastest.
Arguments:
- amplitudes: bfloat16 [512, 512, 256], P('row', 'col'), may hold values from -6 to 6
- integrals: bfloat16 [512, 512, 256], P('row', 'col'), may hold values from -0.0625 to 0.0625
- occ_energy: float32 [16], replicated, may hold values from -1.5 to -0.5
- vir_energy: float32 [512], replicated, may hold values from 0.5 to 3
Outputs:
- updated: float32 [512, 512, 256], P('row', 'col')
The draws below stay inside these ranges and needn't reach their ends.
All inputs are finite; a program needn't handle non-finite values.
Results may differ from the reference program's by a relative error of at most 0.0017.
Values may be sent and summed in bfloat16 or wider, within the bound.
No kernel may reach another device: no remote copies, remote signals or barrier semaphores. Data moves between devices by JAX's collectives and lax.ppermute only.
A program may use at most 192 MiB of HBM per device.

```python
import jax
import jax.numpy as jnp
from jax import lax

VIRT = 512
OCC = 16


def level_of(own_key, shape, pieces, least, largest):
    level, own = 1.0, jax.random.fold_in(own_key, 6)
    for axis_at, parts in pieces:
        steps = jnp.exp(jax.random.uniform(jax.random.fold_in(own, axis_at), (parts,), jnp.float32, least / len(pieces), largest / len(pieces)))
        level = level * jnp.repeat(steps, shape[axis_at] // parts).reshape([-1 if axis == axis_at else 1 for axis in range(len(shape))])
    return level


def normal_values(own_key, dims, width, bound, cuts=(), dtype=jnp.bfloat16):
    level = level_of(own_key, dims, cuts, -0.22, 0.18) if cuts else 1.0
    values = jax.random.normal(own_key, dims, jnp.float32) * width * level
    return jnp.minimum(jnp.maximum(values, -bound), bound).astype(dtype)


def setup_inputs(seed: int = 0) -> dict:
    key_of = jax.random.split(jax.random.key(seed), 5)
    amplitudes = normal_values(key_of[0], (VIRT, VIRT, OCC * OCC), 1.0, 6.0, ((0, 8), (1, 4)))
    integrals = normal_values(key_of[1], (VIRT, VIRT, OCC * OCC), (VIRT * OCC) ** -0.5, 0.0625, ((0, 8), (1, 4)))
    occ_energy = jnp.clip(jax.random.uniform(key_of[2], (OCC,), jnp.float32, -1.5, -0.5), -1.5, -0.5)
    vir_energy = jnp.clip(jax.random.uniform(key_of[3], (VIRT,), jnp.float32, 0.5, 3.0), 0.5, 3.0)
    return {"amplitudes": amplitudes, "integrals": integrals, "occ_energy": occ_energy, "vir_energy": vir_energy}


def reference(amplitudes, integrals, occ_energy, vir_energy):
    amp_full = amplitudes.astype(jnp.float32).reshape(VIRT, VIRT, OCC, OCC)
    int_full = integrals.astype(jnp.float32).reshape(VIRT, VIRT, OCC, OCC)
    cycle_term = jnp.einsum("acik,cbkj->abij", amp_full, int_full, precision=lax.Precision.HIGHEST)
    antisym = cycle_term - cycle_term.transpose(0, 1, 3, 2)
    resid_term = antisym - antisym.transpose(1, 0, 2, 3)
    denominator = (occ_energy[None, None, :, None] + occ_energy[None, None, None, :]
                   - vir_energy[:, None, None, None] - vir_energy[None, :, None, None])
    result = amp_full + resid_term / denominator
    return result.reshape(VIRT, VIRT, OCC * OCC)
```

```python
import jax
import jax.numpy as jnp
import numpy as np
from jax import lax
from jax.sharding import PartitionSpec as P

OCC = 16
CHUNKS = (10, 4, 2)


def local(amplitudes, integrals, occ_energy, vir_energy, rows, cols):
    block_a, block_b, pair_count = amplitudes.shape
    chips = rows // 2
    row_pos = lax.axis_index("row")
    col_pos = lax.axis_index("col")
    chip, core = row_pos // 2, row_pos % 2
    swap = [(r, r ^ 1) for r in range(rows)]

    amp = amplitudes.reshape(block_a, block_b, OCC, OCC).transpose(2, 3, 0, 1)
    ints = integrals.reshape(block_a, block_b, OCC, OCC).transpose(3, 2, 0, 1)

    amp_all = jnp.zeros((OCC, OCC, block_a, cols * block_b), amp.dtype)
    for step in range(cols):
        piece = amp if step == 0 else lax.ppermute(amp, "col", [(q, q ^ step) for q in range(cols)])
        amp_all = lax.dynamic_update_slice(amp_all, piece, (0, 0, 0, (col_pos ^ step) * block_b))

    cycles, starts, first = [], [], 0
    previous = None
    diffs, pairs, mirrors = [], [], []
    mirror_of = [((z * 2 + h) * cols + p, (p * 2 + h) * cols + z)
                 for z in range(chips) for h in range(2) for p in range(cols)]
    for width in CHUNKS:
        own = ints[first:first + width]
        if previous is not None:
            own, previous = lax.optimization_barrier((own, previous))
        blocks = jnp.zeros((width, OCC, rows * block_a, block_b), ints.dtype)

        def put(blocks, value, blk):
            other = lax.ppermute(value, "row", swap)
            blocks = lax.dynamic_update_slice(blocks, value, (0, 0, (blk * 2 + core) * block_a, 0))
            return lax.dynamic_update_slice(blocks, other, (0, 0, (blk * 2 + 1 - core) * block_a, 0))

        blocks = put(blocks, own, chip)
        down, up = [own], [own]
        for step in range(chips - 1):
            down.append(lax.ppermute(down[-1], "row", [
                (2 * z + h, 2 * z - 2 + h) for z in range(1, chips) if z + step < chips for h in range(2)]))
            up.append(lax.ppermute(up[-1], "row", [
                (2 * z + h, 2 * z + 2 + h) for z in range(chips - 1) if z - step >= 0 for h in range(2)]))
        for step in range(chips - 1):
            value = jnp.where(chip + 1 + step < chips, down[step + 1], up[chips - 1 - step])
            blocks = put(blocks, value, (chip + 1 + step) % chips)
        previous = down[-1]
        cycle = jnp.einsum("ikac,jkcb->jiab", amp_all, blocks, preferred_element_type=jnp.float32)
        cycles.append(cycle)
        starts.append(first)
        left, right = [], []
        for j in range(first, first + width):
            if j == 0:
                continue
            left.append(cycle[j - first, :j])
            for begin, earlier in zip(starts, cycles):
                stop = min(j, begin + earlier.shape[0])
                if stop > begin:
                    right.append(earlier[:stop - begin, j])
            pairs += [(i, j) for i in range(j)]
        diff = jnp.concatenate(left) - jnp.concatenate(right)
        diffs.append(diff)
        sent = lax.ppermute(diff.astype(jnp.bfloat16), ("row", "col"), mirror_of)
        other = lax.ppermute(sent, "row", swap)
        low = jnp.where(core == 0, sent, other)
        high = jnp.where(core == 0, other, sent)
        both = jnp.concatenate([low, high], axis=1)
        mirrors.append(lax.dynamic_slice_in_dim(both, core * block_a, block_a, axis=2))
        first += width

    resid = jnp.concatenate(diffs) - jnp.concatenate(mirrors).transpose(0, 2, 1).astype(jnp.float32)
    place = np.full((OCC, OCC), 2 * len(pairs))
    for at, (i, j) in enumerate(pairs):
        place[i, j], place[j, i] = at, len(pairs) + at
    planes = jnp.concatenate([resid, -resid, jnp.zeros_like(resid[:1])])
    full = jnp.take(planes, place.reshape(-1), axis=0).transpose(1, 2, 0)

    vir_rows = lax.dynamic_slice_in_dim(vir_energy, row_pos * block_a, block_a)
    vir_cols = lax.dynamic_slice_in_dim(vir_energy, col_pos * block_b, block_b)
    denominator = (
        (occ_energy[:, None] + occ_energy[None, :]).reshape(1, 1, pair_count)
        - vir_rows[:, None, None]
        - vir_cols[None, :, None]
    )
    return amplitudes.astype(jnp.float32) + full / denominator


def solution(mesh):
    rows, cols = mesh.shape["row"], mesh.shape["col"]
    placed = (P("row", "col", None), P("row", "col", None), P(), P())
    return jax.shard_map(
        lambda *args: local(*args, rows, cols),
        mesh=mesh, in_specs=placed, out_specs=P("row", "col", None), check_vma=False,
    )
```

```python
import functools

import jax
import jax.numpy as jnp
import numpy as np
from jax import lax
from jax.experimental import pallas as pl
from jax.experimental.pallas import tpu as pltpu
from jax.sharding import PartitionSpec as P

OCC = 16
HALF = OCC // 2
CHUNKS = (8, 4, 2, 2)


def diff_kernel(first, earlier_firsts, *refs):
    current, earlier = refs[0], refs[1:1 + len(earlier_firsts)]
    outs = refs[1 + len(earlier_firsts):]
    at = 0
    for j in range(first, first + current.shape[0]):
        if j == 0:
            continue
        for begin, count, source, rows in (
            [(f, e.shape[0], e, first) for f, e in zip(earlier_firsts, earlier)]
            + [(first, j - first, current, 0)]
        ):
            if count == 0:
                continue

            def body(n, carry, begin=begin, source=source, rows=rows, j=j, at=at):
                for who, out in enumerate(outs):
                    out[at + n] = current[j - first, who, begin + n] - source[n, who, j - rows]
                return carry

            lax.fori_loop(0, count, body, 0)
            at += count


def diff_call(first, chunk, cycles, firsts):
    width, _, _, block_a, block_b = chunk.shape
    count = sum(range(first, first + width))
    shape = jax.ShapeDtypeStruct((count, block_a, block_b), jnp.float32)
    in_specs = [pl.BlockSpec(chunk.shape, lambda i: (0,) * 5)]
    for c in cycles:
        in_specs.append(pl.BlockSpec((c.shape[0], 2, width, block_a, block_b),
                                     lambda i: (0, 0, first // width, 0, 0)))
    out_spec = pl.BlockSpec(shape.shape, lambda i: (0, 0, 0))
    return pl.pallas_call(
        functools.partial(diff_kernel, first, tuple(firsts)),
        grid=(1,), out_shape=(shape, shape), in_specs=in_specs, out_specs=(out_spec, out_spec),
        compiler_params=pltpu.CompilerParams(vmem_limit_bytes=60 * 1024 * 1024),
        cost_estimate=pl.CostEstimate(flops=count * block_a * block_b * 2,
                                      bytes_accessed=count * block_a * block_b * 24, transcendentals=0),
    )(chunk, *cycles)


def resid_kernel(core_ref, diff_ref, near_ref, far_ref, out_ref):
    core = core_ref[0]
    block_a = near_ref.shape[1]
    row = lax.broadcasted_iota(jnp.int32, (block_a, 2 * block_a), 0)
    column = lax.broadcasted_iota(jnp.int32, (block_a, 2 * block_a), 1)
    pick = (column == row + core * block_a).astype(jnp.bfloat16)
    lower = core == 0

    def body(n, carry):
        near, far = near_ref[n], far_ref[n]
        rows = jnp.concatenate([jnp.where(lower, near, far), jnp.where(lower, far, near)], axis=0)
        turned = lax.dot_general(pick, rows, (((1,), (1,)), ((), ())), preferred_element_type=jnp.float32)
        out_ref[n] = diff_ref[n] - turned
        return carry

    lax.fori_loop(0, diff_ref.shape[0], body, 0)


def resid_call(core, diff, near, far):
    whole = lambda x: pl.BlockSpec(x.shape, lambda i, s: (0,) * x.ndim)
    return pl.pallas_call(
        resid_kernel, out_shape=jax.ShapeDtypeStruct(diff.shape, jnp.float32),
        grid_spec=pltpu.PrefetchScalarGridSpec(
            num_scalar_prefetch=1, grid=(1,), in_specs=[whole(diff), whole(near), whole(far)],
            out_specs=whole(diff)),
        compiler_params=pltpu.CompilerParams(vmem_limit_bytes=40 * 1024 * 1024),
        cost_estimate=pl.CostEstimate(flops=diff.size * 256, bytes_accessed=diff.size * 12, transcendentals=0),
    )(core.reshape(1), diff, near, far)


def local(amplitudes, integrals, occ_energy, vir_energy, rows, cols):
    block_a, block_b, pair_count = amplitudes.shape
    chips = rows // 2
    row_pos = lax.axis_index("row")
    col_pos = lax.axis_index("col")
    chip, core = row_pos // 2, row_pos % 2
    swap = [(r, r ^ 1) for r in range(rows)]

    def to_core(x):
        return lax.ppermute(x, "row", swap)

    def halves(x):
        keep = lax.dynamic_slice_in_dim(x, core * HALF, HALF, axis=1)
        give = lax.dynamic_slice_in_dim(x, (1 - core) * HALF, HALF, axis=1)
        return keep, to_core(give)

    ints = integrals.reshape(block_a, block_b, OCC, OCC).transpose(3, 2, 0, 1)
    amps = amplitudes.reshape(block_a, block_b, OCC, OCC).transpose(2, 3, 0, 1)
    mine, other = halves(amps)
    own_amp = jnp.stack([mine, other])
    pieces = [own_amp]
    for step in range(1, cols):
        def hop(x, bits):
            return lax.ppermute(x, "col", [(q, q ^ bits) for q in range(cols)])
        if step == 3:
            pieces.append((hop(pieces[1][0], 2), hop(pieces[2][1], 1)))
        else:
            pieces.append(hop(own_amp, step))
    amp_all = jnp.zeros((2, OCC, chips * HALF, block_a, block_b), amps.dtype)
    for step, piece in enumerate(pieces):
        place = (((col_pos ^ step) - chip) % chips) * HALF
        for who, part in ([(0, piece)] if not isinstance(piece, tuple) else enumerate(piece)):
            part = part if part.ndim == 5 else part[None]
            amp_all = lax.dynamic_update_slice(amp_all, part, (who, 0, place, 0, 0))
    amp_all = amp_all.reshape(2 * OCC, chips * HALF, block_a, block_b)

    mirror_of = [((z * 2 + h) * cols + p, (p * 2 + h) * cols + z)
                 for z in range(chips) for h in range(2) for p in range(cols)]
    first, previous = 0, None
    cycles, firsts, resids, pairs = [], [], [], []
    for width in CHUNKS:
        mine, other = halves(ints[first:first + width])
        own = jnp.concatenate([jnp.where(core == 0, mine, other), jnp.where(core == 0, other, mine)], axis=2)
        if previous is not None:
            own, _ = lax.optimization_barrier((own, previous))
        down, up = [own], [own]
        for step in range(chips - 1):
            down.append(lax.ppermute(down[-1], "row", [
                (2 * z + h, 2 * z - 2 + h) for z in range(1, chips) if z + step < chips for h in range(2)]))
            up.append(lax.ppermute(up[-1], "row", [
                (2 * z + h, 2 * z + 2 + h) for z in range(chips - 1) if z - step >= 0 for h in range(2)]))
        previous = (down[-2], up[-2])
        blocks = jnp.concatenate(
            [own] + [jnp.where(chip + step < chips, down[step], up[chips - step]) for step in range(1, chips)],
            axis=1)
        cycle = jnp.einsum("mkac,jkcb->jmab", amp_all, blocks, preferred_element_type=jnp.float32)
        cycle = cycle.reshape(width, 2, OCC, block_a, block_b)
        keep, give = diff_call(first, cycle, cycles, firsts)
        cycles.append(cycle)
        firsts.append(first)
        pairs += [(i, j) for j in range(first, first + width) for i in range(j)]
        diff = keep + to_core(give)
        near = lax.ppermute(diff.astype(jnp.bfloat16), ("row", "col"), mirror_of)
        resids.append(resid_call(core, diff, near, to_core(near)))
        first += width

    expand = np.zeros((len(pairs), pair_count), np.float32)
    for at, (i, j) in enumerate(pairs):
        expand[at, i * OCC + j], expand[at, j * OCC + i] = 1, -1
    resid = jnp.concatenate(resids).transpose(1, 2, 0)
    full = jnp.einsum("abp,pq->abq", resid, jnp.asarray(expand), precision=lax.Precision.HIGHEST)

    vir_rows = lax.dynamic_slice_in_dim(vir_energy, row_pos * block_a, block_a)
    vir_cols = lax.dynamic_slice_in_dim(vir_energy, col_pos * block_b, block_b)
    denominator = (
        (occ_energy[:, None] + occ_energy[None, :]).reshape(1, 1, pair_count)
        - vir_rows[:, None, None]
        - vir_cols[None, :, None]
    )
    return amplitudes.astype(jnp.float32) + full / denominator


def solution(mesh):
    rows, cols = mesh.shape["row"], mesh.shape["col"]
    placed = (P("row", "col", None), P("row", "col", None), P(), P())
    return jax.shard_map(
        lambda *args: local(*args, rows, cols),
        mesh=mesh, in_specs=placed, out_specs=P("row", "col", None), check_vma=False,
    )
```

```python
import functools

import jax
import jax.numpy as jnp
import numpy as np
from jax import lax
from jax.experimental import pallas as pl
from jax.experimental.layout import Layout, with_layout_constraint
from jax.experimental.pallas import tpu as pltpu
from jax.sharding import PartitionSpec as P

OCC = 16
HALF = OCC // 2
CHUNKS = (12, 4)


def diff_kernel(first, earlier_firsts, *refs):
    current, earlier, out = refs[0], refs[1:-1], refs[-1]
    at = 0
    for j in range(first, first + current.shape[0]):
        sources = [(f, e.shape[0], e, first) for f, e in zip(earlier_firsts, earlier)]
        for begin, count, source, rows in sources + [(first, j - first, current, 0)]:
            if count == 0:
                continue

            def body(n, carry, begin=begin, source=source, rows=rows, j=j, at=at):
                out[at + n] = current[j - first, begin + n] - source[n, j - rows]
                return carry

            lax.fori_loop(0, count, body, 0)
            at += count


def diff_call(first, chunk, cycles, firsts):
    width, _, block_a, block_b = chunk.shape
    count = sum(range(first, first + width))
    shape = jax.ShapeDtypeStruct((count, block_a, block_b), jnp.float32)
    in_specs = [pl.BlockSpec(chunk.shape, lambda i: (0,) * 4)]
    for c in cycles:
        in_specs.append(pl.BlockSpec((c.shape[0], width, block_a, block_b),
                                     lambda i: (0, first // width, 0, 0)))
    return pl.pallas_call(
        functools.partial(diff_kernel, first, tuple(firsts)),
        grid=(1,), out_shape=shape, in_specs=in_specs, out_specs=pl.BlockSpec(shape.shape, lambda i: (0, 0, 0)),
        compiler_params=pltpu.CompilerParams(vmem_limit_bytes=40 * 1024 * 1024),
        cost_estimate=pl.CostEstimate(flops=count * block_a * block_b,
                                      bytes_accessed=count * block_a * block_b * 12, transcendentals=0),
    )(chunk, *cycles)


def resid_kernel(core_ref, diff_ref, near_ref, far_ref, out_ref):
    core = core_ref[0]
    block_a = near_ref.shape[1]
    row = lax.broadcasted_iota(jnp.int32, (block_a, 2 * block_a), 0)
    column = lax.broadcasted_iota(jnp.int32, (block_a, 2 * block_a), 1)
    pick = (column == row + core * block_a).astype(jnp.bfloat16)
    lower = core == 0

    def body(n, carry):
        near, far = near_ref[n], far_ref[n]
        rows = jnp.concatenate([jnp.where(lower, near, far), jnp.where(lower, far, near)], axis=0)
        turned = lax.dot_general(pick, rows, (((1,), (1,)), ((), ())), preferred_element_type=jnp.float32)
        out_ref[n] = diff_ref[n] - turned
        return carry

    lax.fori_loop(0, diff_ref.shape[0], body, 0)


def resid_call(core, diff, near, far):
    whole = lambda x: pl.BlockSpec(x.shape, lambda i, s: (0,) * x.ndim)
    return pl.pallas_call(
        resid_kernel, out_shape=jax.ShapeDtypeStruct(diff.shape, jnp.float32),
        grid_spec=pltpu.PrefetchScalarGridSpec(
            num_scalar_prefetch=1, grid=(1,), in_specs=[whole(diff), whole(near), whole(far)],
            out_specs=whole(diff)),
        compiler_params=pltpu.CompilerParams(vmem_limit_bytes=40 * 1024 * 1024),
        cost_estimate=pl.CostEstimate(flops=diff.size * 256, bytes_accessed=diff.size * 12, transcendentals=0),
    )(core.reshape(1), diff, near, far)


def turns_of(chips, cols):
    if chips == cols == 4:
        return [{(0, 3), (1, 2), (2, 3), (3, 0)}, {(2, 1), (1, 0)}]
    return []


def local(amplitudes, integrals, occ_energy, vir_energy, rows, cols):
    block_a, block_b, pair_count = amplitudes.shape
    chips = rows // 2
    row_pos = lax.axis_index("row")
    col_pos = lax.axis_index("col")
    core = row_pos % 2
    swap = [(r, r ^ 1) for r in range(rows)]

    def to_core(x):
        return lax.ppermute(x, "row", swap)

    def planes(x):
        return with_layout_constraint(x, Layout(major_to_minor=(0, 1, 2, 3)))

    ints = planes(integrals.reshape(block_a, block_b, OCC, OCC).transpose(2, 3, 0, 1))
    gathered, first = [], 0
    for width in CHUNKS:
        gathered.append(lax.all_gather(planes(ints[:, first:first + width]), "row", axis=2, tiled=True))
        first += width

    amps = planes(amplitudes.reshape(block_a, block_b, OCC, OCC).transpose(2, 3, 0, 1))

    def hop(x, bits):
        return lax.ppermute(x, "col", [(q, q ^ bits) for q in range(cols)])

    parts = (amps[:HALF], amps[HALF:])
    pieces = [parts]
    for step in range(1, cols):
        if step == 3:
            pieces.append((hop(pieces[1][0], 2), hop(pieces[2][1], 1)))
        else:
            pieces.append(tuple(hop(x, step) for x in parts))
    amp_all = jnp.zeros((OCC, OCC, block_a, cols * block_b), amps.dtype)
    for step, piece in enumerate(pieces):
        place = (col_pos ^ step) * block_b
        for n, part in enumerate([amps] if step == 0 else piece):
            amp_all = lax.dynamic_update_slice(amp_all, part, (n * HALF, 0, 0, place))

    at = lambda z, h, p: (z * 2 + h) * cols + p
    flows = [(z, h, p) for z in range(chips) for h in range(2) for p in range(cols)]
    turns = turns_of(chips, cols)
    direct = [(at(z, h, p), at(p, h, z)) for z, h, p in flows if not any((z, p) in t for t in turns)]

    def to_mirror(x):
        out = lax.ppermute(x, ("row", "col"), direct)
        for turn in turns:
            across = [(at(z, h, p), at(z, h, z)) for z, h, p in flows if (z, p) in turn]
            along = [(at(z, h, z), at(p, h, z)) for z, h, p in flows if (z, p) in turn]
            moved = lax.ppermute(x, ("row", "col"), across)
            out = out + lax.ppermute(moved, ("row", "col"), along)
        return out

    first, ready = 0, None
    cycles, firsts, resids, pairs = [], [], [], []
    for width, blocks in zip(CHUNKS, gathered):
        if ready is not None:
            blocks, _ = lax.optimization_barrier((blocks, ready))
        cycle = jnp.einsum("ikac,kjcb->jiab", amp_all, blocks, preferred_element_type=jnp.float32)
        diff = diff_call(first, cycle, cycles, firsts)
        cycles.append(cycle)
        firsts.append(first)
        pairs += [(i, j) for j in range(first, first + width) for i in range(j)]
        ready = diff.astype(jnp.bfloat16)
        near = to_mirror(ready)
        resids.append(resid_call(core, diff, near, to_core(near)))
        first += width

    expand = np.zeros((len(pairs), pair_count), np.float32)
    for at, (i, j) in enumerate(pairs):
        expand[at, i * OCC + j], expand[at, j * OCC + i] = 1, -1
    resid = jnp.concatenate(resids).transpose(1, 2, 0)
    full = jnp.einsum("abp,pq->abq", resid, jnp.asarray(expand), precision=lax.Precision.HIGHEST)

    vir_rows = lax.dynamic_slice_in_dim(vir_energy, row_pos * block_a, block_a)
    vir_cols = lax.dynamic_slice_in_dim(vir_energy, col_pos * block_b, block_b)
    denominator = (
        (occ_energy[:, None] + occ_energy[None, :]).reshape(1, 1, pair_count)
        - vir_rows[:, None, None]
        - vir_cols[None, :, None]
    )
    return amplitudes.astype(jnp.float32) + full / denominator


def solution(mesh):
    rows, cols = mesh.shape["row"], mesh.shape["col"]
    placed = (P("row", "col", None), P("row", "col", None), P(), P())

    def body(*args):
        return local(*args, rows, cols)

    return jax.shard_map(body, mesh=mesh, in_specs=placed, out_specs=P("row", "col", None), check_vma=False)
```

```python
import functools

import jax
import jax.numpy as jnp
import numpy as np
from jax import lax
from jax.experimental import pallas as pl
from jax.experimental.layout import Layout, with_layout_constraint
from jax.experimental.pallas import tpu as pltpu
from jax.sharding import PartitionSpec as P

OCC = 16
HALF = OCC // 2
CHUNKS = (14, 2)


def diff_kernel(first, earlier_firsts, *refs):
    current, earlier, out, sent = refs[0], refs[1:-2], refs[-2], refs[-1]
    at = 0
    for j in range(first, first + current.shape[0]):
        sources = [(f, e.shape[0], e, first if e.shape[1] < OCC else 0) for f, e in zip(earlier_firsts, earlier)]
        for begin, count, source, rows in sources + [(first, j - first, current, 0)]:
            if count == 0:
                continue

            def body(n, carry, begin=begin, source=source, rows=rows, j=j, at=at):
                value = current[j - first, begin + n] - source[n, j - rows]
                out[at + n] = value
                sent[at + n] = value.astype(sent.dtype)
                return carry

            lax.fori_loop(0, count, body, 0)
            at += count


def diff_call(first, chunk, cycles, firsts):
    width, _, block_a, block_b = chunk.shape
    count = sum(range(first, first + width))
    shape = jax.ShapeDtypeStruct((count, block_a, block_b), jnp.float32)
    in_specs = [pl.BlockSpec(chunk.shape, lambda i: (0,) * 4)]
    aligned = first % width == 0
    for c in cycles:
        in_specs.append(pl.BlockSpec((c.shape[0], width if aligned else OCC, block_a, block_b),
                                     lambda i: (0, first // width if aligned else 0, 0, 0)))
    return pl.pallas_call(
        functools.partial(diff_kernel, first, tuple(firsts)),
        grid=(1,), out_shape=(shape, jax.ShapeDtypeStruct(shape.shape, jnp.bfloat16)), in_specs=in_specs,
        out_specs=(pl.BlockSpec(shape.shape, lambda i: (0, 0, 0)),) * 2,
        compiler_params=pltpu.CompilerParams(vmem_limit_bytes=40 * 1024 * 1024),
        cost_estimate=pl.CostEstimate(flops=count * block_a * block_b,
                                      bytes_accessed=count * block_a * block_b * 14, transcendentals=0),
    )(chunk, *cycles)


def resid_kernel(core_ref, diff_ref, near_ref, far_ref, out_ref):
    core = core_ref[0]
    block_a = near_ref.shape[1]
    row = lax.broadcasted_iota(jnp.int32, (block_a, 2 * block_a), 0)
    column = lax.broadcasted_iota(jnp.int32, (block_a, 2 * block_a), 1)
    pick = (column == row + core * block_a).astype(jnp.bfloat16)
    lower = core == 0

    def turn(n):
        near, far = near_ref[n], far_ref[n]
        rows = jnp.concatenate([jnp.where(lower, near, far), jnp.where(lower, far, near)], axis=0)
        turned = lax.dot_general(pick, rows, (((1,), (1,)), ((), ())), preferred_element_type=jnp.float32)
        out_ref[n] = diff_ref[n] - turned

    count, together = diff_ref.shape[0], 6

    def body(n, carry):
        for m in range(together):
            turn(n * together + m)
        return carry

    lax.fori_loop(0, count // together, body, 0)
    for n in range(count - count % together, count):
        turn(n)


def resid_call(core, diff, near, far):
    whole = lambda x: pl.BlockSpec(x.shape, lambda i, s: (0,) * x.ndim)
    return pl.pallas_call(
        resid_kernel, out_shape=jax.ShapeDtypeStruct(diff.shape, jnp.float32),
        grid_spec=pltpu.PrefetchScalarGridSpec(
            num_scalar_prefetch=1, grid=(1,), in_specs=[whole(diff), whole(near), whole(far)],
            out_specs=whole(diff)),
        compiler_params=pltpu.CompilerParams(vmem_limit_bytes=40 * 1024 * 1024),
        cost_estimate=pl.CostEstimate(flops=diff.size * 256, bytes_accessed=diff.size * 12, transcendentals=0),
    )(core.reshape(1), diff, near, far)


def turns_of(chips, cols):
    if chips == cols == 4:
        return [{(0, 3), (1, 2), (2, 3), (3, 0)}, {(2, 1), (1, 0)}]
    return []


def local(amplitudes, integrals, occ_energy, vir_energy, rows, cols):
    block_a, block_b, pair_count = amplitudes.shape
    chips = rows // 2
    row_pos = lax.axis_index("row")
    col_pos = lax.axis_index("col")
    core = row_pos % 2
    swap = [(r, r ^ 1) for r in range(rows)]

    def to_core(x):
        return lax.ppermute(x, "row", swap)

    def planes(x):
        return with_layout_constraint(x, Layout(major_to_minor=(0, 1, 2, 3)))

    ints = planes(integrals.reshape(block_a, block_b, OCC, OCC).transpose(2, 3, 0, 1))
    gathered, first = [], 0
    for width in CHUNKS:
        gathered.append(lax.all_gather(planes(ints[:, first:first + width]), "row", axis=2, tiled=True))
        first += width

    amps = planes(amplitudes.reshape(block_a, block_b, OCC, OCC).transpose(2, 3, 0, 1))

    def hop(x, bits):
        return lax.ppermute(x, "col", [(q, q ^ bits) for q in range(cols)])

    parts = (amps[:HALF], amps[HALF:])
    pieces = [parts]
    for step in range(1, cols):
        if step == 3:
            pieces.append((hop(pieces[1][0], 2), hop(pieces[2][1], 1)))
        else:
            pieces.append(tuple(hop(x, step) for x in parts))
    amp_all = jnp.zeros((OCC, OCC, block_a, cols * block_b), amps.dtype)
    for step, piece in enumerate(pieces):
        place = (col_pos ^ step) * block_b
        for n, part in enumerate([amps] if step == 0 else piece):
            amp_all = lax.dynamic_update_slice(amp_all, part, (n * HALF, 0, 0, place))

    at = lambda z, h, p: (z * 2 + h) * cols + p
    flows = [(z, h, p) for z in range(chips) for h in range(2) for p in range(cols)]

    def to_mirror(x, at_chunk):
        turns = turns_of(chips, cols) if at_chunk + 1 < len(CHUNKS) else []
        direct = [(at(z, h, p), at(p, h, z)) for z, h, p in flows if not any((z, p) in t for t in turns)]
        arrivals = [lax.ppermute(x, ("row", "col"), direct)]
        for turn in turns:
            across = [(at(z, h, p), at(z, h, z)) for z, h, p in flows if (z, p) in turn]
            along = [(at(z, h, z), at(p, h, z)) for z, h, p in flows if (z, p) in turn]
            moved = lax.ppermute(x, ("row", "col"), across)
            arrivals.append(lax.ppermute(moved, ("row", "col"), along))
        return arrivals

    first, ready = 0, None
    cycles, firsts, mirrors, pairs = [], [], [], []
    for at_chunk, (width, blocks) in enumerate(zip(CHUNKS, gathered)):
        if ready is not None:
            blocks, _ = lax.optimization_barrier((blocks, ready))
        cycle = jnp.einsum("ikac,kjcb->jiab", amp_all, blocks, preferred_element_type=jnp.float32)
        diff, ready = diff_call(first, cycle, cycles, firsts)
        cycles.append(cycle)
        firsts.append(first)
        pairs += [(i, j) for j in range(first, first + width) for i in range(j)]
        mirrors.append((diff, to_mirror(ready, at_chunk)))
        first += width

    resids = []
    for diff, arrivals in mirrors:
        near = sum(arrivals[1:], arrivals[0])
        resids.append(resid_call(core, diff, near, to_core(near)))

    expand = np.zeros((len(pairs), pair_count), np.float32)
    for at, (i, j) in enumerate(pairs):
        expand[at, i * OCC + j], expand[at, j * OCC + i] = 1, -1
    resid = jnp.concatenate(resids).transpose(1, 2, 0)
    full = jnp.einsum("abp,pq->abq", resid, jnp.asarray(expand), precision=lax.Precision.HIGHEST)

    vir_rows = lax.dynamic_slice_in_dim(vir_energy, row_pos * block_a, block_a)
    vir_cols = lax.dynamic_slice_in_dim(vir_energy, col_pos * block_b, block_b)
    denominator = (
        (occ_energy[:, None] + occ_energy[None, :]).reshape(1, 1, pair_count)
        - vir_rows[:, None, None]
        - vir_cols[None, :, None]
    )
    return amplitudes.astype(jnp.float32) + full / denominator


def solution(mesh):
    rows, cols = mesh.shape["row"], mesh.shape["col"]
    placed = (P("row", "col", None), P("row", "col", None), P(), P())

    def body(*args):
        return local(*args, rows, cols)

    return jax.shard_map(body, mesh=mesh, in_specs=placed, out_specs=P("row", "col", None), check_vma=False)
```

```python
import functools

import jax
import jax.numpy as jnp
import numpy as np
from jax import lax
from jax.experimental import pallas as pl
from jax.experimental.layout import Layout, with_layout_constraint
from jax.experimental.pallas import tpu as pltpu
from jax.sharding import PartitionSpec as P

OCC = 16
HALF = OCC // 2
GATHERS = (14, 2)
CHUNKS = (11, 3, 2)


def diff_kernel(first, earlier_firsts, *refs):
    current, earlier, out, sent = refs[0], refs[1:-2], refs[-2], refs[-1]
    at = 0
    for j in range(first, first + current.shape[0]):
        sources = [(f, e.shape[0], e, first if e.shape[1] < OCC else 0) for f, e in zip(earlier_firsts, earlier)]
        for begin, count, source, rows in sources + [(first, j - first, current, 0)]:
            if count == 0:
                continue

            def body(n, carry, begin=begin, source=source, rows=rows, j=j, at=at):
                value = current[j - first, begin + n] - source[n, j - rows]
                out[at + n] = value
                sent[at + n] = value.astype(sent.dtype)
                return carry

            lax.fori_loop(0, count, body, 0)
            at += count


def diff_call(first, chunk, cycles, firsts):
    width, _, block_a, block_b = chunk.shape
    count = sum(range(first, first + width))
    shape = jax.ShapeDtypeStruct((count, block_a, block_b), jnp.float32)
    in_specs = [pl.BlockSpec(chunk.shape, lambda i: (0,) * 4)]
    aligned = first % width == 0
    for c in cycles:
        in_specs.append(pl.BlockSpec((c.shape[0], width if aligned else OCC, block_a, block_b),
                                     lambda i: (0, first // width if aligned else 0, 0, 0)))
    return pl.pallas_call(
        functools.partial(diff_kernel, first, tuple(firsts)),
        grid=(1,), out_shape=(shape, jax.ShapeDtypeStruct(shape.shape, jnp.bfloat16)), in_specs=in_specs,
        out_specs=(pl.BlockSpec(shape.shape, lambda i: (0, 0, 0)),) * 2,
        compiler_params=pltpu.CompilerParams(vmem_limit_bytes=40 * 1024 * 1024),
        cost_estimate=pl.CostEstimate(flops=count * block_a * block_b,
                                      bytes_accessed=count * block_a * block_b * 14, transcendentals=0),
    )(chunk, *cycles)


def resid_kernel(core_ref, diff_ref, near_ref, far_ref, out_ref):
    core = core_ref[0]
    block_a = near_ref.shape[1]
    row = lax.broadcasted_iota(jnp.int32, (block_a, 2 * block_a), 0)
    column = lax.broadcasted_iota(jnp.int32, (block_a, 2 * block_a), 1)
    pick = (column == row + core * block_a).astype(jnp.bfloat16)
    lower = core == 0

    def turn(n):
        near, far = near_ref[n], far_ref[n]
        rows = jnp.concatenate([jnp.where(lower, near, far), jnp.where(lower, far, near)], axis=0)
        turned = lax.dot_general(pick, rows, (((1,), (1,)), ((), ())), preferred_element_type=jnp.float32)
        out_ref[n] = diff_ref[n] - turned

    count, together = diff_ref.shape[0], 6

    def body(n, carry):
        for m in range(together):
            turn(n * together + m)
        return carry

    lax.fori_loop(0, count // together, body, 0)
    for n in range(count - count % together, count):
        turn(n)


def resid_call(core, diff, near, far):
    whole = lambda x: pl.BlockSpec(x.shape, lambda i, s: (0,) * x.ndim)
    return pl.pallas_call(
        resid_kernel, out_shape=jax.ShapeDtypeStruct(diff.shape, jnp.float32),
        grid_spec=pltpu.PrefetchScalarGridSpec(
            num_scalar_prefetch=1, grid=(1,), in_specs=[whole(diff), whole(near), whole(far)],
            out_specs=whole(diff)),
        compiler_params=pltpu.CompilerParams(vmem_limit_bytes=40 * 1024 * 1024),
        cost_estimate=pl.CostEstimate(flops=diff.size * 256, bytes_accessed=diff.size * 12, transcendentals=0),
    )(core.reshape(1), diff, near, far)


def turns_of(chips, cols):
    if chips == cols == 4:
        return [{(0, 3), (1, 2), (2, 3), (3, 0)}, {(2, 1), (1, 0)}]
    return []


def local(amplitudes, integrals, occ_energy, vir_energy, rows, cols):
    block_a, block_b, pair_count = amplitudes.shape
    chips = rows // 2
    row_pos = lax.axis_index("row")
    col_pos = lax.axis_index("col")
    core = row_pos % 2
    swap = [(r, r ^ 1) for r in range(rows)]

    def to_core(x):
        return lax.ppermute(x, "row", swap)

    def planes(x):
        return with_layout_constraint(x, Layout(major_to_minor=(0, 1, 2, 3)))

    ints = planes(integrals.reshape(block_a, block_b, OCC, OCC).transpose(2, 3, 0, 1))
    gathered, first = [], 0
    for width in GATHERS:
        gathered.append(
            (first, lax.all_gather(planes(ints[:, first:first + width]), "row", axis=2, tiled=True)))
        first += width

    amps = planes(amplitudes.reshape(block_a, block_b, OCC, OCC).transpose(2, 3, 0, 1))

    def hop(x, bits):
        return lax.ppermute(x, "col", [(q, q ^ bits) for q in range(cols)])

    parts = (amps[:HALF], amps[HALF:])
    pieces = [parts]
    for step in range(1, cols):
        if step == 3:
            pieces.append((hop(pieces[1][0], 2), hop(pieces[2][1], 1)))
        else:
            pieces.append(tuple(hop(x, step) for x in parts))
    amp_all = jnp.zeros((OCC, OCC, block_a, cols * block_b), amps.dtype)
    for step, piece in enumerate(pieces):
        place = (col_pos ^ step) * block_b
        for n, part in enumerate([amps] if step == 0 else piece):
            amp_all = lax.dynamic_update_slice(amp_all, part, (n * HALF, 0, 0, place))

    at = lambda z, h, p: (z * 2 + h) * cols + p
    flows = [(z, h, p) for z in range(chips) for h in range(2) for p in range(cols)]

    def to_mirror(x, at_chunk):
        turns = turns_of(chips, cols) if at_chunk + 1 < len(CHUNKS) else []
        direct = [(at(z, h, p), at(p, h, z)) for z, h, p in flows if not any((z, p) in t for t in turns)]
        arrivals = [lax.ppermute(x, ("row", "col"), direct)]
        for turn in turns:
            across = [(at(z, h, p), at(z, h, z)) for z, h, p in flows if (z, p) in turn]
            along = [(at(z, h, z), at(p, h, z)) for z, h, p in flows if (z, p) in turn]
            moved = lax.ppermute(x, ("row", "col"), across)
            arrivals.append(lax.ppermute(moved, ("row", "col"), along))
        return arrivals

    first, ready = 0, None
    cycles, firsts, mirrors, pairs = [], [], [], []
    for at_chunk, width in enumerate(CHUNKS):
        begin, blocks = [g for g in gathered if g[0] <= first][-1]
        if ready is not None:
            blocks, _ = lax.optimization_barrier((blocks, ready))
        cycle = jnp.einsum("ikac,kjcb->jiab", amp_all, blocks[:, first - begin:first - begin + width],
                           preferred_element_type=jnp.float32)
        diff, ready = diff_call(first, cycle, cycles, firsts)
        cycles.append(cycle)
        firsts.append(first)
        pairs += [(i, j) for j in range(first, first + width) for i in range(j)]
        mirrors.append((diff, to_mirror(ready, at_chunk)))
        first += width

    resids = []
    for diff, arrivals in mirrors:
        near = sum(arrivals[1:], arrivals[0])
        resids.append(resid_call(core, diff, near, to_core(near)))

    expand = np.zeros((len(pairs), pair_count), np.float32)
    for at, (i, j) in enumerate(pairs):
        expand[at, i * OCC + j], expand[at, j * OCC + i] = 1, -1
    resid = jnp.concatenate(resids).transpose(1, 2, 0)
    full = jnp.einsum("abp,pq->abq", resid, jnp.asarray(expand), precision=lax.Precision.HIGH)

    vir_rows = lax.dynamic_slice_in_dim(vir_energy, row_pos * block_a, block_a)
    vir_cols = lax.dynamic_slice_in_dim(vir_energy, col_pos * block_b, block_b)
    denominator = (
        (occ_energy[:, None] + occ_energy[None, :]).reshape(1, 1, pair_count)
        - vir_rows[:, None, None]
        - vir_cols[None, :, None]
    )
    return amplitudes.astype(jnp.float32) + full / denominator


def solution(mesh):
    rows, cols = mesh.shape["row"], mesh.shape["col"]
    placed = (P("row", "col", None), P("row", "col", None), P(), P())

    def body(*args):
        return local(*args, rows, cols)

    return jax.shard_map(body, mesh=mesh, in_specs=placed, out_specs=P("row", "col", None), check_vma=False)
```
